32 devices in a mesh: groups: 2 (over x), src: 16 (over z, y, core).
Axes of the slice: x: 2, y: 2, z: 4, core: 2. Of those that a mesh axis runs over, the one named last changes fastest.
Arguments:
- eigenvectors: bfloat16 [32, 2, 3, 16, 8, 4, 128], P('groups', None, None, 'src'), parts along dimension 0, may hold values from -0.71875 to 0.71875
- gauge_links: bfloat16 [32, 2, 2, 3, 3, 16, 8, 4], P('groups', None, None, None, None, 'src'), parts along dimension 0, may hold values from -2.5 to 2.5
- hop_path: int32 [4], P('groups'), parts along dimension 0, may hold values from 0 to 3, as said below
- spin_perm: int32 [4, 4], P('groups'), parts along dimension 0, may hold values from 0 to 3, each once within a row
- spin_phase: int32 [4, 4], P('groups'), parts along dimension 0, may hold values from 0 to 3
- perambulators: bfloat16 [32, 2, 512, 512], P('groups', None, 'src'), parts along dimension 0, may hold values from -0.1875 to 0.1875
- owned_times: int32 [32, 2], P('groups'), parts along dimension 0, may hold values from -1 to 15, as said below
Outputs:
- insertions: bfloat16 [64, 2, 2, 512, 512], P(('groups', 'src')), parts along dimension 0
The draws below stay inside these ranges and needn't reach their ends.
There are 2 independent parts, one for each index of `groups`. The reference program is written for one: setup_inputs(seed, part) draws one part's arguments, and reference() takes and returns one part's arrays. A program takes and returns all parts, laid end to end along the dimension named above; each array names one. Nothing has to cross between parts.
Inputs may be any that keep to these rules, and one draw needn't show every extreme that they name: `hop_path`: codes 0, 1, 2, 3 stand for +y, -y, +z, -z; the 2 codes of the path are all different. `spin_perm`: each row is a permutation of the 4 spins. `owned_times`: every sink time 0 to 15 appears exactly once; a row lists its times first and then -1; a row lists at most 2 times, and some row exactly 2.
All inputs are finite; a program needn't handle non-finite values.
Results may differ from the reference program's by a relative error of at most 0.0058.
Values may be sent and summed in bfloat16 or wider, within the bound.
A program may use at most 128 MiB of HBM per device.

```python
import jax
import jax.numpy as jnp
from jax import lax

NVEC = 128
SPINS = 4
LY = 8
LZ = 4
NHOP = 2
NG = 2
TPD = 1
MOST = 2
LX = 16
NT = 16
N_SRC = 16


def draw_hop_path(key, part):
    base = jax.random.fold_in(key, 11)
    order = jax.random.permutation(base, 4).astype(jnp.int32)
    return order[:NHOP].astype(jnp.int32)


def draw_owned_times(key, part):
    base = jax.random.fold_in(key, 7)
    rank_key, time_key = jax.random.split(base)
    rank_order = jax.random.permutation(rank_key, N_SRC)
    heavy_count = N_SRC // 4
    counts = jnp.where(rank_order < heavy_count, MOST, jnp.where(rank_order < 2 * heavy_count, 0, TPD)).astype(jnp.int32)
    starts = jnp.cumsum(counts) - counts
    shuffled = jax.random.permutation(time_key, NT).astype(jnp.int32)
    slot_index = jnp.arange(MOST, dtype=jnp.int32)
    position = starts[:, None] + slot_index[None, :]
    picked = shuffled[jnp.clip(position, 0, NT - 1)]
    return jnp.where(slot_index[None, :] < counts[:, None], picked, -1).astype(jnp.int32)


def plant(drawn, key, low, top_value):
    spot = [jax.random.randint(jax.random.fold_in(key, axis), (), 0, length) for axis, length in enumerate(drawn.shape)]
    main_axis = drawn.shape.index(max(drawn.shape))
    neighbour = spot[:main_axis] + [(spot[main_axis] + 1) % drawn.shape[main_axis]] + spot[main_axis + 1:]
    return drawn.at[tuple(spot)].set(low).at[tuple(neighbour)].set(top_value)


def shard_levels(rng, dims, cuts, least, high):
    factor_of = 1.0
    for dim, shards_of in cuts:
        heights = jax.random.uniform(jax.random.fold_in(jax.random.fold_in(rng, 6), dim), (shards_of,), jnp.float32, least / len(cuts), high / len(cuts))
        factor_of = factor_of * jnp.repeat(jnp.exp(heights), dims[dim] // shards_of).reshape((-1,) + (1,) * (len(dims) - 1 - dim))
    return factor_of


def gaussian(rng, dims, deviation, bound, pieces=(), kind=jnp.bfloat16):
    factor_of = shard_levels(rng, dims, pieces, -0.22, 0.18) if pieces else 1.0
    result = jax.random.normal(rng, dims, jnp.float32) * deviation * factor_of
    return jnp.minimum(jnp.maximum(result, -bound), bound).astype(kind)


def setup_inputs(seed: int = 0, part: int = 0) -> dict:
    arg_keys = jax.random.split(jax.random.key(seed), 8)
    own_keys = jax.random.split(jax.random.fold_in(arg_keys[7], part), 8)
    return {
        "eigenvectors": gaussian(own_keys[0], (NT, 2, 3, LX, LY, LZ, NVEC), 0.12, 0.71875, ((3, 16),)),
        "gauge_links": gaussian(own_keys[1], (NT, 2, 2, 3, 3, LX, LY, LZ), 6 ** -0.5, 2.5, ((5, 16),)),
        "hop_path": draw_hop_path(jax.random.fold_in(jax.random.fold_in(arg_keys[7], part), 71), part),
        "spin_perm": jax.vmap(lambda own: jax.random.permutation(own, SPINS))(jax.random.split(own_keys[3], NG)).reshape((NG, SPINS)).astype(jnp.int32),
        "spin_phase": plant(jax.random.randint(own_keys[4], (NG, SPINS), 0, 4), jax.random.fold_in(own_keys[4], 1), 0, 3).astype(jnp.int32),
        "perambulators": gaussian(own_keys[5], (NT, 2, SPINS * NVEC, SPINS * NVEC), (2 * SPINS * NVEC) ** -0.5, 0.1875, ((2, 16),)),
        "owned_times": draw_owned_times(jax.random.fold_in(jax.random.fold_in(arg_keys[7], part), 71), part),
    }


def select_four(direction, first_case, second_case, third_case, fourth_case):
    return jnp.where(direction == 0, first_case, jnp.where(direction == 1, second_case, jnp.where(direction == 2, third_case, fourth_case)))


def adjoint(matrix):
    return jnp.stack([jnp.swapaxes(matrix[:, 0], 1, 2), -jnp.swapaxes(matrix[:, 1], 1, 2)], 1)


def displace(vectors, gauge_links, direction):
    forward_y = gauge_links[:, 0]
    forward_z = gauge_links[:, 1]
    link_pick = select_four(direction, forward_y, adjoint(jnp.roll(forward_y, 1, 5)), forward_z, adjoint(jnp.roll(forward_z, 1, 6)))
    displaced = select_four(direction, jnp.roll(vectors, -1, 4), jnp.roll(vectors, 1, 4), jnp.roll(vectors, -1, 5), jnp.roll(vectors, 1, 5))
    link_re = link_pick[:, 0].astype(jnp.float32)
    link_im = link_pick[:, 1].astype(jnp.float32)
    moved_re = displaced[:, 0].astype(jnp.float32)
    moved_im = displaced[:, 1].astype(jnp.float32)
    form = 'tcdxyz,tdxyzn->tcxyzn'
    real_part = jnp.einsum(form, link_re, moved_re) - jnp.einsum(form, link_im, moved_im)
    imag_part = jnp.einsum(form, link_re, moved_im) + jnp.einsum(form, link_im, moved_re)
    return lax.optimization_barrier(jnp.stack([real_part, imag_part], 1).astype(jnp.bfloat16))


def triple(stored, elemental, spin_perm, phase_re, phase_im):
    order = SPINS * NVEC
    stored_f = stored.astype(jnp.float32)
    columns = stored_f.reshape(2, order, SPINS, NVEC)
    permuted = jnp.take(columns, spin_perm, axis=2)
    products = jnp.einsum('kab,jdgsb->kjgdsa', elemental.astype(jnp.float32), permuted)
    real_part = products[0, 0] - products[1, 1]
    imag_part = products[0, 1] + products[1, 0]
    scale_re = phase_re[:, None, :, None]
    scale_im = phase_im[:, None, :, None]
    inserted = jnp.stack([scale_re * real_part - scale_im * imag_part, scale_re * imag_part + scale_im * real_part], 0)
    inserted = lax.optimization_barrier(inserted.reshape(2, NG, order, order).astype(jnp.bfloat16))
    outer = jnp.einsum('kcr,jgdr->kjgcd', stored_f, inserted.astype(jnp.float32))
    return jnp.stack([outer[0, 0] + outer[1, 1], outer[0, 1] - outer[1, 0]], 1).astype(jnp.bfloat16)


def reference(eigenvectors, gauge_links, hop_path, spin_perm, spin_phase, perambulators, owned_times):
    shifted = eigenvectors
    for hop_index in range(NHOP):
        shifted = displace(shifted, gauge_links, hop_path[hop_index])
    eigen_rows = eigenvectors.reshape(NT, 2, -1, NVEC).astype(jnp.float32)
    moved_rows = shifted.reshape(NT, 2, -1, NVEC).astype(jnp.float32)
    products = jnp.einsum('tkra,tjrb->tkjab', eigen_rows, moved_rows)
    elemental = jnp.stack([products[:, 0, 0] + products[:, 1, 1], products[:, 0, 1] - products[:, 1, 0]], 1)
    elemental = lax.optimization_barrier(elemental.astype(jnp.bfloat16))
    phase_re = (spin_phase == 0).astype(jnp.float32) - (spin_phase == 2).astype(jnp.float32)
    phase_im = (spin_phase == 1).astype(jnp.float32) - (spin_phase == 3).astype(jnp.float32)

    def one_time(time_pair):
        return triple(time_pair[0], time_pair[1], spin_perm, phase_re, phase_im)

    per_time = lax.map(one_time, (perambulators, elemental))
    slot_times = owned_times.reshape(-1)
    picked = jnp.take(per_time, jnp.clip(slot_times, 0, NT - 1).astype(jnp.int32), axis=0)
    filled = (slot_times >= 0)[:, None, None, None, None]
    return jnp.where(filled, picked, jnp.zeros_like(picked))
```

```python
import functools

import jax
import jax.numpy as jnp
from jax import lax
from jax.experimental import pallas as pl
from jax.experimental.pallas import tpu as pltpu
from jax.sharding import PartitionSpec as P

F32 = jnp.float32
BF16 = jnp.bfloat16
QUAD = 4


def hop_tables(gauge_links, hop_path):
    time_count, side_y, side_z = gauge_links.shape[0], gauge_links.shape[6], gauge_links.shape[7]
    sites = side_y * side_z
    links = gauge_links.reshape(time_count, 2, 2, 3, 3, sites)
    site = jnp.arange(sites)
    ypos, zpos = site // side_z, site % side_z
    up_y = ((ypos + 1) % side_y) * side_z + zpos
    up_z = ypos * side_z + (zpos + 1) % side_z
    step_up = jnp.where((hop_path < 2)[:, None], up_y[None], up_z[None])
    minus = (hop_path % 2) == 1
    up = (step_up[:, :, None] == site[None, None, :]).astype(BF16)
    mask = jnp.where(minus[:, None, None], jnp.swapaxes(up, 1, 2), up)
    axis = jnp.where((hop_path < 2)[None, :, None, None, None, None], links[:, None, 0], links[:, None, 1])
    mover = jnp.where(minus[:, None, None], jnp.eye(sites, dtype=BF16)[None], up)
    moved = jnp.einsum("thkcdx,hxy->thkcdy", axis, mover, preferred_element_type=F32)
    flipped = jnp.swapaxes(moved, 3, 4) * jnp.array([1.0, -1.0], F32)[None, None, :, None, None, None]
    rows = jnp.where(minus[None, :, None, None, None, None], flipped, moved)
    rows = rows.reshape(time_count, hop_path.shape[0], 6, 3 * sites)
    return rows, jnp.tile(mask.astype(F32), (1, 1, 3))


def exchange_kernel(
    n, hops, times_ref, pera_ref, eig_ref, rows_ref, mask_ref,
    blocks_ref, elem_ref,
    pstage, epart, estage, erecv, fstage, frecv,
    psend, precv, plocal, qsend, qrecv, zsend, zrecv,
):
    me = lax.axis_index("src")
    slots = blocks_ref.shape[0]
    time_count = eig_ref.shape[0]
    rings = n // QUAD
    mine_q, mine_z = lax.rem(me, QUAD), me // QUAD

    barrier = pltpu.get_barrier_semaphore()

    @pl.loop(1, n)
    def _(o):
        pl.semaphore_signal(barrier, inc=1, device_id={"src": lax.rem(me + o, n)})

    @pl.loop(0, n)
    def _(d):
        for s in range(slots):
            pstage[d, s] = pera_ref[times_ref[d * slots + s]]

    pl.semaphore_wait(barrier, n - 1)

    def pera_copy(o, s, origin):
        peer = lax.rem(me + o, n)
        return pltpu.make_async_remote_copy(
            src_ref=pstage.at[peer, s], dst_ref=blocks_ref.at[s, origin],
            send_sem=psend.at[s, o], recv_sem=precv.at[s, o], device_id={"src": peer},
        )

    for s in range(slots):
        pltpu.make_async_copy(pstage.at[me, s], blocks_ref.at[s, me], plocal.at[s]).start()

    def send_slot(s):
        @pl.loop(1, n)
        def _(o):
            pera_copy(o, s, me).start()

    send_slot(0)

    def one_time(t, carry):
        vec = eig_ref[t]
        cur = vec
        half = vec.shape[0] // 2
        for h in range(hops):
            mask = mask_ref[h]
            row = rows_ref[t, h]
            re = jnp.concatenate([mask * row[c : c + 1] for c in range(3)], 0)
            im = jnp.concatenate([mask * row[3 + c : 4 + c] for c in range(3)], 0)
            re, im, neg = re.astype(BF16), im.astype(BF16), (-im).astype(BF16)
            top, low = cur[:half], cur[half:]
            out_re = jnp.dot(re, top, preferred_element_type=F32) + jnp.dot(neg, low, preferred_element_type=F32)
            out_im = jnp.dot(im, top, preferred_element_type=F32) + jnp.dot(re, low, preferred_element_type=F32)
            cur = jnp.concatenate([out_re, out_im], 0).astype(BF16)
        turned = jnp.concatenate([cur[half:], -cur[:half]], 0)
        both = jnp.concatenate([cur, turned], 1)
        part = lax.dot_general(vec, both, (((0,), (0,)), ((), ())), preferred_element_type=F32)
        epart[t] = part.astype(BF16)
        return carry

    lax.fori_loop(0, time_count, one_time, 0, unroll=4)

    @pl.loop(0, rings)
    def _(z):
        for q in range(QUAD):
            for s in range(slots):
                estage[q, z * slots + s] = epart[times_ref[(z * QUAD + q) * slots + s]]

    def quad_copy(o, origin):
        peer = lax.rem(mine_q + o, QUAD)
        return pltpu.make_async_remote_copy(
            src_ref=estage.at[peer], dst_ref=erecv.at[origin],
            send_sem=qsend.at[o], recv_sem=qrecv.at[o], device_id={"src": mine_z * QUAD + peer},
        )

    for o in range(1, QUAD):
        quad_copy(o, mine_q).start()
    for s in range(1, slots):
        send_slot(s)
    for o in range(1, QUAD):
        quad_copy(o, lax.rem(mine_q + QUAD - o, QUAD)).wait()

    @pl.loop(0, rings * slots)
    def _(j):
        total = estage[mine_q, j].astype(F32)
        for o in range(1, QUAD):
            total += erecv[lax.rem(mine_q + o, QUAD), j].astype(F32)
        fstage[j // slots, lax.rem(j, slots)] = total.astype(BF16)

    def ring_copy(o, origin):
        peer = lax.rem(mine_z + o, rings)
        return pltpu.make_async_remote_copy(
            src_ref=fstage.at[peer], dst_ref=frecv.at[origin],
            send_sem=zsend.at[o], recv_sem=zrecv.at[o], device_id={"src": peer * QUAD + mine_q},
        )

    for o in range(1, rings):
        ring_copy(o, mine_z).start()
    for o in range(1, rings):
        ring_copy(o, lax.rem(mine_z + rings - o, rings)).wait()
    total = fstage[mine_z].astype(F32)
    for o in range(1, rings):
        total += frecv[lax.rem(mine_z + o, rings)].astype(F32)
    elem_ref[...] = total.astype(BF16)

    for s in range(slots):
        pltpu.make_async_copy(pstage.at[me, s], blocks_ref.at[s, me], plocal.at[s]).wait()

        @pl.loop(1, n)
        def _(o):
            pera_copy(o, s, lax.rem(me + n - o, n)).wait()


def triple_kernel(perm_ref, phase_ref, mine_ref, blocks_ref, elem_ref, out_ref, left, turned):
    slot, group = pl.program_id(0), pl.program_id(1)
    order = out_ref.shape[-1]
    width = elem_ref.shape[1]
    spins = order // width

    @pl.when(group == 0)
    def _():
        elem = elem_ref[0]
        re = blocks_ref[0, :, 0].reshape(order, order)
        im = blocks_ref[0, :, 1].reshape(order, order)
        left[:, :order] = re
        left[:, order:] = im
        for spin in range(spins):
            part_re = re[:, spin * width : (spin + 1) * width]
            part_im = im[:, spin * width : (spin + 1) * width]
            dims = (((1,), (1,)), ((), ()))
            turned[spin, 0] = lax.dot_general(
                elem, jnp.concatenate([part_re, -part_im], 1), dims, preferred_element_type=F32
            ).astype(BF16)
            turned[spin, 1] = lax.dot_general(
                elem, jnp.concatenate([part_im, part_re], 1), dims, preferred_element_type=F32
            ).astype(BF16)

    reals, imags = [], []
    for spin in range(spins):
        source = perm_ref[group, spin]
        phase = phase_ref[group, spin]
        scale_re = (phase == 0).astype(F32) - (phase == 2).astype(F32)
        scale_im = (phase == 1).astype(F32) - (phase == 3).astype(F32)
        re = turned[source, 0].astype(F32)
        im = turned[source, 1].astype(F32)
        reals.append((scale_re * re - scale_im * im).astype(BF16))
        imags.append((scale_re * im + scale_im * re).astype(BF16))
    real, imag = jnp.concatenate(reals, 0), jnp.concatenate(imags, 0)
    filled = mine_ref[slot] >= 0
    lhs = left[...]
    for part, right in enumerate((jnp.concatenate([real, imag], 0), jnp.concatenate([imag, -real], 0))):
        result = jnp.dot(lhs, right, preferred_element_type=F32)
        out_ref[0, 0, part] = jnp.where(filled, result, 0.0).astype(BF16)


def shards(n, eigenvectors, gauge_links, hop_path, spin_perm, spin_phase, perambulators, owned_times):
    time_count = eigenvectors.shape[0]
    width = eigenvectors.shape[-1]
    slots = owned_times.shape[1]
    rows, order = perambulators.shape[2], perambulators.shape[3]
    groups = spin_perm.shape[0]
    hops = hop_path.shape[0]
    rings = n // QUAD
    listed = jnp.clip(owned_times.reshape(-1), 0, time_count - 1)
    mine = lax.dynamic_index_in_dim(owned_times, lax.axis_index("src"), 0, keepdims=False)
    eig = eigenvectors.reshape(time_count, -1, width)
    link_rows, mask = hop_tables(gauge_links, hop_path)
    vmem = pl.BlockSpec(memory_space=pltpu.VMEM)
    smem = pl.BlockSpec(memory_space=pltpu.SMEM)
    blocks, elem = pl.pallas_call(
        functools.partial(exchange_kernel, n, hops),
        out_shape=(
            jax.ShapeDtypeStruct((slots, n, 2, rows, order), BF16),
            jax.ShapeDtypeStruct((slots, width, 2 * width), BF16),
        ),
        in_specs=[smem, vmem, vmem, vmem, vmem],
        out_specs=(pl.BlockSpec(memory_space=pl.ANY), vmem),
        scratch_shapes=[
            pltpu.VMEM((n, slots, 2, rows, order), BF16),
            pltpu.VMEM((time_count, width, 2 * width), BF16),
            pltpu.VMEM((QUAD, rings * slots, width, 2 * width), BF16),
            pltpu.VMEM((QUAD, rings * slots, width, 2 * width), BF16),
            pltpu.VMEM((rings, slots, width, 2 * width), BF16),
            pltpu.VMEM((rings, slots, width, 2 * width), BF16),
            pltpu.SemaphoreType.DMA((slots, n)),
            pltpu.SemaphoreType.DMA((slots, n)),
            pltpu.SemaphoreType.DMA((slots,)),
            pltpu.SemaphoreType.DMA((QUAD,)),
            pltpu.SemaphoreType.DMA((QUAD,)),
            pltpu.SemaphoreType.DMA((rings,)),
            pltpu.SemaphoreType.DMA((rings,)),
        ],
        compiler_params=pltpu.CompilerParams(
            collective_id=0, has_side_effects=True, vmem_limit_bytes=48 * 2**20
        ),
        name="exchange",
    )(listed, perambulators, eig, link_rows, mask)
    return pl.pallas_call(
        triple_kernel,
        grid=(slots, groups),
        out_shape=jax.ShapeDtypeStruct((slots, groups, 2, order, order), BF16),
        in_specs=[
            smem,
            smem,
            smem,
            pl.BlockSpec((1, n, 2, rows, order), lambda s, g: (s, 0, 0, 0, 0)),
            pl.BlockSpec((1, width, 2 * width), lambda s, g: (s, 0, 0)),
        ],
        out_specs=pl.BlockSpec((1, 1, 2, order, order), lambda s, g: (s, g, 0, 0, 0)),
        scratch_shapes=[
            pltpu.VMEM((order, 2 * order), BF16),
            pltpu.VMEM((order // width, 2, width, order), BF16),
        ],
        compiler_params=pltpu.CompilerParams(
            dimension_semantics=("arbitrary", "arbitrary"), vmem_limit_bytes=40 * 2**20
        ),
        name="triple",
    )(spin_perm, spin_phase, mine, blocks, elem)


def solution(mesh):
    in_specs = (
        P("groups", None, None, "src", None, None, None),
        P("groups", None, None, None, None, "src", None, None),
        P("groups"),
        P("groups", None),
        P("groups", None),
        P("groups", None, "src", None),
        P("groups", None),
    )
    out_specs = P(("groups", "src"), None, None, None, None)
    return jax.shard_map(
        functools.partial(shards, mesh.shape["src"]),
        mesh=mesh, in_specs=in_specs, out_specs=out_specs, check_vma=False,
    )
```

```python
import functools

import jax
import jax.numpy as jnp
import numpy as np
from jax import lax
from jax.experimental import pallas as pl
from jax.experimental.pallas import tpu as pltpu
from jax.sharding import PartitionSpec as P

F32 = jnp.float32
BF16 = jnp.bfloat16
QUAD = 4


def site_tables(side_y, side_z):
    sites = side_y * side_z
    site = np.arange(sites)
    ypos, zpos = site // side_z, site % side_z
    up_y = ((ypos + 1) % side_y) * side_z + zpos
    up_z = ypos * side_z + (zpos + 1) % side_z
    masks, movers = [], []
    for target in (up_y, up_z):
        up = (target[:, None] == site[None, :]).astype(np.float32)
        masks += [up, up.T]
        movers += [up, np.eye(sites, dtype=np.float32)]
    masks = np.stack([np.tile(m, (1, 3)) for m in masks])
    movers = np.stack([np.kron(np.eye(3, dtype=np.float32), m) for m in movers])
    return masks, movers


def exchange_kernel(
    n, hops, owned_ref, hop_ref, pera_ref, eig_ref, links_ref, masks_ref, movers_ref,
    blocks_ref, elem_ref,
    pstage, epart, rows_ref, hopmask, sends, recvs, keeps,
    psend, precv, plocal, esend, erecv,
):
    me = lax.axis_index("src")
    slots = blocks_ref.shape[0]
    time_count = eig_ref.shape[0]
    rings = n // QUAD
    stages = n.bit_length() - 1
    mine_q, mine_z = lax.rem(me, QUAD), me // QUAD

    def listed(d, s):
        return jnp.minimum(jnp.maximum(owned_ref[d, s], 0), time_count - 1)

    barrier = pltpu.get_barrier_semaphore()

    @pl.loop(1, n)
    def _(o):
        pl.semaphore_signal(barrier, inc=1, device_id={"src": lax.rem(me + o, n)})

    @pl.loop(0, n)
    def _(d):
        for s in range(slots):
            pstage[d, s] = pera_ref[listed(d, s)]

    pl.semaphore_wait(barrier, n - 1)

    def pera_copy(dz, dq, s, receive):
        peer = lax.rem(mine_z + dz, rings) * QUAD + lax.rem(mine_q + dq, QUAD)
        source = lax.rem(mine_z + rings - dz, rings) * QUAD + lax.rem(mine_q + QUAD - dq, QUAD)
        return pltpu.make_async_remote_copy(
            src_ref=pstage.at[peer, s], dst_ref=blocks_ref.at[s, source if receive else me],
            send_sem=psend.at[s, dz, dq], recv_sem=precv.at[s, dz, dq], device_id={"src": peer},
        )

    def local_copy(s):
        return pltpu.make_async_copy(pstage.at[me, s], blocks_ref.at[s, me], plocal.at[s])

    def send_far(s):
        @pl.loop(0, rings - 1)
        def _(i):
            dz = lax.rem(i + rings // 2 - 1, rings - 1) + 1
            for dq in range(QUAD):
                pera_copy(dz, dq, s, False).start()

    def send_near(s):
        local_copy(s).start()
        for dq in range(1, QUAD):
            pera_copy(0, dq, s, False).start()

    def wait_slot(s):
        @pl.loop(0, rings - 1)
        def _(i):
            for dq in range(QUAD):
                pera_copy(i + 1, dq, s, True).wait()

        for dq in range(1, QUAD):
            pera_copy(0, dq, s, True).wait()
        local_copy(s).wait()

    send_far(0)

    for h in range(hops):
        code = hop_ref[h]
        pick = [(code == i).astype(F32) for i in range(4)]
        hopmask[h] = sum(pick[i] * masks_ref[i] for i in range(4))
        mover = sum(pick[i] * movers_ref[i] for i in range(4)).astype(BF16)
        for k in range(2):
            sign = 1.0 - 2.0 * k
            for c in range(3):
                stack = []
                for d in range(3):
                    here, flip = k * 9 + c * 3 + d, k * 9 + d * 3 + c
                    stack.append(
                        pick[0] * links_ref[here].astype(F32)
                        + (sign * pick[1]) * links_ref[flip].astype(F32)
                        + pick[2] * links_ref[18 + here].astype(F32)
                        + (sign * pick[3]) * links_ref[18 + flip].astype(F32)
                    )
                rows_ref[h, k * 3 + c] = lax.dot_general(
                    jnp.concatenate(stack, 0).astype(BF16), mover, (((0,), (0,)), ((), ())),
                    preferred_element_type=F32,
                )

    def one_time(t, carry):
        vec = eig_ref[t]
        cur = vec
        half = vec.shape[0] // 2
        for h in range(hops):
            mask = hopmask[h]
            row = [rows_ref[h, i, pl.ds(t, 1), :] for i in range(6)]
            re = jnp.concatenate([mask * row[c] for c in range(3)], 0)
            im = jnp.concatenate([mask * row[3 + c] for c in range(3)], 0)
            re, im, neg = re.astype(BF16), im.astype(BF16), (-im).astype(BF16)
            top, low = cur[:half], cur[half:]
            out_re = jnp.dot(re, top, preferred_element_type=F32) + jnp.dot(neg, low, preferred_element_type=F32)
            out_im = jnp.dot(im, top, preferred_element_type=F32) + jnp.dot(re, low, preferred_element_type=F32)
            cur = jnp.concatenate([out_re, out_im], 0).astype(BF16)
        turned = jnp.concatenate([cur[half:], -cur[:half]], 0)
        both = jnp.concatenate([cur, turned], 1)
        epart[t] = lax.dot_general(vec, both, (((0,), (0,)), ((), ())), preferred_element_type=F32)
        return carry

    lax.fori_loop(0, time_count, one_time, 0, unroll=4)

    for s in range(1, slots):
        send_far(s)

    def elem_copy(b):
        bit = lax.rem(me // (1 << b), 2)
        return pltpu.make_async_remote_copy(
            src_ref=sends[b], dst_ref=recvs[b], send_sem=esend.at[b], recv_sem=erecv.at[b],
            device_id={"src": me + (1 << b) * (1 - 2 * bit)},
        )

    for b in range(stages):
        bit = lax.rem(me // (1 << b), 2)
        count = n >> (b + 1)

        def value(i, s, b=b):
            if b == 0:
                return epart[listed(i, s)]
            return keeps[b - 1][i, s] + recvs[b - 1][i, s].astype(F32)

        @pl.loop(0, count)
        def _(i):
            for s in range(slots):
                sends[b][i, s] = value(2 * i + 1 - bit, s).astype(sends[b].dtype)

        elem_copy(b).start()

        @pl.loop(0, count)
        def _(i):
            for s in range(slots):
                keeps[b][i, s] = value(2 * i + bit, s)

        elem_copy(b).wait()
    elem_ref[...] = (keeps[stages - 1][0] + recvs[stages - 1][0].astype(F32)).astype(BF16)

    for s in range(slots):
        send_near(s)
    for s in range(slots):
        wait_slot(s)


def triple_kernel(perm_ref, phase_ref, owned_ref, blocks_ref, elem_ref, out_ref, left, turned):
    slot, group = pl.program_id(0), pl.program_id(1)
    order = out_ref.shape[-1]
    width = elem_ref.shape[1]
    spins = order // width

    @pl.when(group == 0)
    def _():
        elem = elem_ref[0]
        re = blocks_ref[0, :, 0].reshape(order, order)
        im = blocks_ref[0, :, 1].reshape(order, order)
        left[:, :order] = re
        left[:, order:] = im
        for spin in range(spins):
            part_re = re[:, spin * width : (spin + 1) * width]
            part_im = im[:, spin * width : (spin + 1) * width]
            dims = (((1,), (1,)), ((), ()))
            turned[spin, 0] = lax.dot_general(
                elem, jnp.concatenate([part_re, -part_im], 1), dims, preferred_element_type=F32
            ).astype(BF16)
            turned[spin, 1] = lax.dot_general(
                elem, jnp.concatenate([part_im, part_re], 1), dims, preferred_element_type=F32
            ).astype(BF16)

    reals, imags = [], []
    for spin in range(spins):
        source = perm_ref[group, spin]
        phase = phase_ref[group, spin]
        scale_re = (phase == 0).astype(F32) - (phase == 2).astype(F32)
        scale_im = (phase == 1).astype(F32) - (phase == 3).astype(F32)
        re = turned[source, 0].astype(F32)
        im = turned[source, 1].astype(F32)
        reals.append((scale_re * re - scale_im * im).astype(BF16))
        imags.append((scale_re * im + scale_im * re).astype(BF16))
    real, imag = jnp.concatenate(reals, 0), jnp.concatenate(imags, 0)
    filled = owned_ref[lax.axis_index("src"), slot] >= 0
    lhs = left[...]
    for part, right in enumerate((jnp.concatenate([real, imag], 0), jnp.concatenate([imag, -real], 0))):
        result = jnp.dot(lhs, right, preferred_element_type=F32)
        out_ref[0, 0, part] = jnp.where(filled, result, 0.0).astype(BF16)


def shards(n, eigenvectors, gauge_links, hop_path, spin_perm, spin_phase, perambulators, owned_times):
    time_count = eigenvectors.shape[0]
    width = eigenvectors.shape[-1]
    slots = owned_times.shape[1]
    rows, order = perambulators.shape[2], perambulators.shape[3]
    groups = spin_perm.shape[0]
    hops = hop_path.shape[0]
    rings = n // QUAD
    side_y, side_z = eigenvectors.shape[4], eigenvectors.shape[5]
    sites = side_y * side_z
    eig = eigenvectors.reshape(time_count, -1, width)
    links = jnp.transpose(gauge_links.reshape(time_count, 36, sites), (1, 2, 0))
    masks, movers = site_tables(side_y, side_z)
    stages = n.bit_length() - 1
    tile = (slots, width, 2 * width)
    vmem = pl.BlockSpec(memory_space=pltpu.VMEM)
    smem = pl.BlockSpec(memory_space=pltpu.SMEM)
    parts = [pltpu.VMEM((n >> (b + 1),) + tile, F32 if b == 0 else BF16) for b in range(stages)]
    blocks, elem = pl.pallas_call(
        functools.partial(exchange_kernel, n, hops),
        out_shape=(
            jax.ShapeDtypeStruct((slots, n, 2, rows, order), BF16),
            jax.ShapeDtypeStruct(tile, BF16),
        ),
        in_specs=[smem, smem] + [vmem] * 5,
        out_specs=(pl.BlockSpec(memory_space=pl.ANY), vmem),
        scratch_shapes=[
            pltpu.VMEM((n, slots, 2, rows, order), BF16),
            pltpu.VMEM((time_count, width, 2 * width), F32),
            pltpu.VMEM((hops, 6, time_count, 3 * sites), F32),
            pltpu.VMEM((hops, sites, 3 * sites), F32),
            parts,
            parts,
            [pltpu.VMEM((n >> (b + 1),) + tile, F32) for b in range(stages)],
            pltpu.SemaphoreType.DMA((slots, rings, QUAD)),
            pltpu.SemaphoreType.DMA((slots, rings, QUAD)),
            pltpu.SemaphoreType.DMA((slots,)),
            pltpu.SemaphoreType.DMA((stages,)),
            pltpu.SemaphoreType.DMA((stages,)),
        ],
        compiler_params=pltpu.CompilerParams(
            collective_id=0, has_side_effects=True, vmem_limit_bytes=56 * 2**20
        ),
        name="exchange",
    )(owned_times, hop_path, perambulators, eig, links, jnp.asarray(masks), jnp.asarray(movers))
    return pl.pallas_call(
        triple_kernel,
        grid=(slots, groups),
        out_shape=jax.ShapeDtypeStruct((slots, groups, 2, order, order), BF16),
        in_specs=[
            smem,
            smem,
            smem,
            pl.BlockSpec((1, n, 2, rows, order), lambda s, g: (s, 0, 0, 0, 0)),
            pl.BlockSpec((1, width, 2 * width), lambda s, g: (s, 0, 0)),
        ],
        out_specs=pl.BlockSpec((1, 1, 2, order, order), lambda s, g: (s, g, 0, 0, 0)),
        scratch_shapes=[
            pltpu.VMEM((order, 2 * order), BF16),
            pltpu.VMEM((order // width, 2, width, order), BF16),
        ],
        compiler_params=pltpu.CompilerParams(
            dimension_semantics=("arbitrary", "arbitrary"), vmem_limit_bytes=40 * 2**20
        ),
        name="triple",
    )(spin_perm, spin_phase, owned_times, blocks, elem)


def solution(mesh):
    in_specs = (
        P("groups", None, None, "src", None, None, None),
        P("groups", None, None, None, None, "src", None, None),
        P("groups"),
        P("groups", None),
        P("groups", None),
        P("groups", None, "src", None),
        P("groups", None),
    )
    out_specs = P(("groups", "src"), None, None, None, None)
    return jax.shard_map(
        functools.partial(shards, mesh.shape["src"]),
        mesh=mesh, in_specs=in_specs, out_specs=out_specs, check_vma=False,
    )
```

```python
import functools

import jax
import jax.numpy as jnp
import numpy as np
from jax import lax
from jax.experimental import pallas as pl
from jax.experimental.pallas import tpu as pltpu
from jax.sharding import PartitionSpec as P

F32 = jnp.float32
BF16 = jnp.bfloat16
QUAD = 4


def site_tables(side_y, side_z):
    sites = side_y * side_z
    site = np.arange(sites)
    ypos, zpos = site // side_z, site % side_z
    up_y = ((ypos + 1) % side_y) * side_z + zpos
    up_z = ypos * side_z + (zpos + 1) % side_z
    masks, movers = [], []
    for target in (up_y, up_z):
        up = (target[:, None] == site[None, :]).astype(np.float32)
        masks += [up, up.T]
        movers += [up, np.eye(sites, dtype=np.float32)]
    masks = np.stack([np.tile(m, (1, 3)) for m in masks])
    movers = np.stack([np.kron(np.eye(3, dtype=np.float32), m) for m in movers])
    return masks, movers


def exchange_kernel(
    n, hops, owned_ref, hop_ref, pera_hbm, eig_hbm, links_hbm, masks_hbm, movers_hbm,
    blocks_ref, elem_ref,
    pera_ref, eig_ref, links_ref, masks_ref, movers_ref, fetch, pstage, epart, rows_ref, hopmask, estage, erecv, fstage, frecv,
    psend, precv, plocal, qsend, qrecv, zsend, zrecv,
):
    me = lax.axis_index("src")
    slots = blocks_ref.shape[0]
    time_count = eig_ref.shape[0]
    rings = n // QUAD
    mine_q, mine_z = lax.rem(me, QUAD), me // QUAD

    def listed(d, s):
        return jnp.minimum(jnp.maximum(owned_ref[d, s], 0), time_count - 1)

    pairs = (
        (pera_hbm, pera_ref), (eig_hbm, eig_ref), (links_hbm, links_ref),
        (masks_hbm, masks_ref), (movers_hbm, movers_ref),
    )
    fetches = [pltpu.make_async_copy(src, dst, fetch.at[i]) for i, (src, dst) in enumerate(pairs)]
    for copy in fetches:
        copy.start()

    barrier = pltpu.get_barrier_semaphore()

    @pl.loop(1, n)
    def _(o):
        pl.semaphore_signal(barrier, inc=1, device_id={"src": lax.rem(me + o, n)})

    fetches[0].wait()

    @pl.loop(0, n)
    def _(d):
        for s in range(slots):
            pstage[d, s] = pera_ref[listed(d, s)]

    pl.semaphore_wait(barrier, n - 1)

    def pera_copy(dz, dq, s, receive):
        peer = lax.rem(mine_z + dz, rings) * QUAD + lax.rem(mine_q + dq, QUAD)
        source = lax.rem(mine_z + rings - dz, rings) * QUAD + lax.rem(mine_q + QUAD - dq, QUAD)
        return pltpu.make_async_remote_copy(
            src_ref=pstage.at[peer, s], dst_ref=blocks_ref.at[s, source if receive else me],
            send_sem=psend.at[s, dz, dq], recv_sem=precv.at[s, dz, dq], device_id={"src": peer},
        )

    def local_copy(s):
        return pltpu.make_async_copy(pstage.at[me, s], blocks_ref.at[s, me], plocal.at[s])

    def send_slot(s):
        local_copy(s).start()

        @pl.loop(1, n)
        def _(o):
            pera_copy(o // QUAD, lax.rem(o, QUAD), s, False).start()

    def wait_slot(s):
        @pl.loop(0, rings - 1)
        def _(i):
            for dq in range(QUAD):
                pera_copy(i + 1, dq, s, True).wait()

        for dq in range(1, QUAD):
            pera_copy(0, dq, s, True).wait()
        local_copy(s).wait()

    send_slot(0)

    for copy in fetches[1:]:
        copy.wait()
    for h in range(hops):
        code = hop_ref[h]
        pick = [(code == i).astype(F32) for i in range(4)]
        hopmask[h] = sum(pick[i] * masks_ref[i] for i in range(4))
        mover = sum(pick[i] * movers_ref[i] for i in range(4)).astype(BF16)
        for k in range(2):
            sign = 1.0 - 2.0 * k
            for c in range(3):
                stack = []
                for d in range(3):
                    here, flip = k * 9 + c * 3 + d, k * 9 + d * 3 + c
                    stack.append(
                        pick[0] * links_ref[here].astype(F32)
                        + (sign * pick[1]) * links_ref[flip].astype(F32)
                        + pick[2] * links_ref[18 + here].astype(F32)
                        + (sign * pick[3]) * links_ref[18 + flip].astype(F32)
                    )
                rows_ref[h, k * 3 + c] = lax.dot_general(
                    jnp.concatenate(stack, 0).astype(BF16), mover, (((0,), (0,)), ((), ())),
                    preferred_element_type=F32,
                )

    def one_time(t, carry):
        vec = eig_ref[t]
        cur = vec
        half = vec.shape[0] // 2
        for h in range(hops):
            mask = hopmask[h]
            row = [rows_ref[h, i, pl.ds(t, 1), :] for i in range(6)]
            re = jnp.concatenate([mask * row[c] for c in range(3)], 0)
            im = jnp.concatenate([mask * row[3 + c] for c in range(3)], 0)
            re, im, neg = re.astype(BF16), im.astype(BF16), (-im).astype(BF16)
            top, low = cur[:half], cur[half:]
            out_re = jnp.dot(re, top, preferred_element_type=F32) + jnp.dot(neg, low, preferred_element_type=F32)
            out_im = jnp.dot(im, top, preferred_element_type=F32) + jnp.dot(re, low, preferred_element_type=F32)
            cur = jnp.concatenate([out_re, out_im], 0).astype(BF16)
        turned = jnp.concatenate([cur[half:], -cur[:half]], 0)
        both = jnp.concatenate([cur, turned], 1)
        part = lax.dot_general(vec, both, (((0,), (0,)), ((), ())), preferred_element_type=F32)
        epart[t] = part.astype(BF16)
        return carry

    lax.fori_loop(0, time_count, one_time, 0, unroll=4)

    @pl.loop(0, rings)
    def _(z):
        for q in range(QUAD):
            for s in range(slots):
                estage[q, z * slots + s] = epart[listed(z * QUAD + q, s)]

    def quad_copy(o, origin):
        peer = lax.rem(mine_q + o, QUAD)
        return pltpu.make_async_remote_copy(
            src_ref=estage.at[peer], dst_ref=erecv.at[origin],
            send_sem=qsend.at[o], recv_sem=qrecv.at[o], device_id={"src": mine_z * QUAD + peer},
        )

    for o in range(1, QUAD):
        quad_copy(o, mine_q).start()
    for s in range(1, slots):
        send_slot(s)
    for o in range(1, QUAD):
        quad_copy(o, lax.rem(mine_q + QUAD - o, QUAD)).wait()

    @pl.loop(0, rings * slots)
    def _(j):
        total = estage[mine_q, j].astype(F32)
        for o in range(1, QUAD):
            total += erecv[lax.rem(mine_q + o, QUAD), j].astype(F32)
        fstage[j // slots, lax.rem(j, slots)] = total.astype(BF16)

    def ring_copy(o, origin):
        peer = lax.rem(mine_z + o, rings)
        return pltpu.make_async_remote_copy(
            src_ref=fstage.at[peer], dst_ref=frecv.at[origin],
            send_sem=zsend.at[o], recv_sem=zrecv.at[o], device_id={"src": peer * QUAD + mine_q},
        )

    for o in range(1, rings):
        ring_copy(o, mine_z).start()
    for o in range(1, rings):
        ring_copy(o, lax.rem(mine_z + rings - o, rings)).wait()
    total = fstage[mine_z].astype(F32)
    for o in range(1, rings):
        total += frecv[lax.rem(mine_z + o, rings)].astype(F32)
    elem_ref[...] = total.astype(BF16)

    for s in range(slots):
        wait_slot(s)


def triple_kernel(perm_ref, phase_ref, owned_ref, blocks_ref, elem_ref, out_ref, left, turned):
    slot, group = pl.program_id(0), pl.program_id(1)
    order = out_ref.shape[-1]
    width = elem_ref.shape[1]
    spins = order // width

    @pl.when(group == 0)
    def _():
        elem = elem_ref[0]
        re = blocks_ref[0, :, 0].reshape(order, order)
        im = blocks_ref[0, :, 1].reshape(order, order)
        left[:, :order] = re
        left[:, order:] = im
        for spin in range(spins):
            part_re = re[:, spin * width : (spin + 1) * width]
            part_im = im[:, spin * width : (spin + 1) * width]
            dims = (((1,), (1,)), ((), ()))
            turned[spin, 0] = lax.dot_general(
                elem, jnp.concatenate([part_re, -part_im], 1), dims, preferred_element_type=F32
            ).astype(BF16)
            turned[spin, 1] = lax.dot_general(
                elem, jnp.concatenate([part_im, part_re], 1), dims, preferred_element_type=F32
            ).astype(BF16)

    reals, imags = [], []
    for spin in range(spins):
        source = perm_ref[group, spin]
        phase = phase_ref[group, spin]
        scale_re = (phase == 0).astype(F32) - (phase == 2).astype(F32)
        scale_im = (phase == 1).astype(F32) - (phase == 3).astype(F32)
        re = turned[source, 0].astype(F32)
        im = turned[source, 1].astype(F32)
        reals.append((scale_re * re - scale_im * im).astype(BF16))
        imags.append((scale_re * im + scale_im * re).astype(BF16))
    real, imag = jnp.concatenate(reals, 0), jnp.concatenate(imags, 0)
    filled = owned_ref[lax.axis_index("src"), slot] >= 0
    lhs = left[...]
    for part, right in enumerate((jnp.concatenate([real, imag], 0), jnp.concatenate([imag, -real], 0))):
        result = jnp.dot(lhs, right, preferred_element_type=F32)
        out_ref[0, 0, part] = jnp.where(filled, result, 0.0).astype(BF16)


def shards(n, eigenvectors, gauge_links, hop_path, spin_perm, spin_phase, perambulators, owned_times):
    time_count = eigenvectors.shape[0]
    width = eigenvectors.shape[-1]
    slots = owned_times.shape[1]
    rows, order = perambulators.shape[2], perambulators.shape[3]
    groups = spin_perm.shape[0]
    hops = hop_path.shape[0]
    rings = n // QUAD
    side_y, side_z = eigenvectors.shape[4], eigenvectors.shape[5]
    sites = side_y * side_z
    eig = eigenvectors.reshape(time_count, -1, width)
    links = jnp.transpose(gauge_links.reshape(time_count, 36, sites), (1, 2, 0))
    masks, movers = site_tables(side_y, side_z)
    tile = (slots, width, 2 * width)
    vmem = pl.BlockSpec(memory_space=pltpu.VMEM)
    smem = pl.BlockSpec(memory_space=pltpu.SMEM)
    arrays = (perambulators, eig, links, jnp.asarray(masks), jnp.asarray(movers))
    blocks, elem = pl.pallas_call(
        functools.partial(exchange_kernel, n, hops),
        out_shape=(
            jax.ShapeDtypeStruct((slots, n, 2, rows, order), BF16),
            jax.ShapeDtypeStruct(tile, BF16),
        ),
        in_specs=[smem, smem] + [pl.BlockSpec(memory_space=pltpu.HBM)] * 5,
        out_specs=(pl.BlockSpec(memory_space=pl.ANY), vmem),
        scratch_shapes=[pltpu.VMEM(a.shape, a.dtype) for a in arrays]
        + [
            pltpu.SemaphoreType.DMA((len(arrays),)),
            pltpu.VMEM((n, slots, 2, rows, order), BF16),
            pltpu.VMEM((time_count, width, 2 * width), BF16),
            pltpu.VMEM((hops, 6, time_count, 3 * sites), F32),
            pltpu.VMEM((hops, sites, 3 * sites), F32),
            pltpu.VMEM((QUAD, rings * slots, width, 2 * width), BF16),
            pltpu.VMEM((QUAD, rings * slots, width, 2 * width), BF16),
            pltpu.VMEM((rings,) + tile, BF16),
            pltpu.VMEM((rings,) + tile, BF16),
            pltpu.SemaphoreType.DMA((slots, rings, QUAD)),
            pltpu.SemaphoreType.DMA((slots, rings, QUAD)),
            pltpu.SemaphoreType.DMA((slots,)),
            pltpu.SemaphoreType.DMA((QUAD,)),
            pltpu.SemaphoreType.DMA((QUAD,)),
            pltpu.SemaphoreType.DMA((rings,)),
            pltpu.SemaphoreType.DMA((rings,)),
        ],
        compiler_params=pltpu.CompilerParams(
            collective_id=0, has_side_effects=True, vmem_limit_bytes=56 * 2**20
        ),
        name="exchange",
    )(owned_times, hop_path, *arrays)
    return pl.pallas_call(
        triple_kernel,
        grid=(slots, groups),
        out_shape=jax.ShapeDtypeStruct((slots, groups, 2, order, order), BF16),
        in_specs=[
            smem,
            smem,
            smem,
            pl.BlockSpec((1, n, 2, rows, order), lambda s, g: (s, 0, 0, 0, 0)),
            pl.BlockSpec((1, width, 2 * width), lambda s, g: (s, 0, 0)),
        ],
        out_specs=pl.BlockSpec((1, 1, 2, order, order), lambda s, g: (s, g, 0, 0, 0)),
        scratch_shapes=[
            pltpu.VMEM((order, 2 * order), BF16),
            pltpu.VMEM((order // width, 2, width, order), BF16),
        ],
        compiler_params=pltpu.CompilerParams(
            dimension_semantics=("arbitrary", "arbitrary"), vmem_limit_bytes=56 * 2**20
        ),
        name="triple",
    )(spin_perm, spin_phase, owned_times, blocks, elem)


def solution(mesh):
    in_specs = (
        P("groups", None, None, "src", None, None, None),
        P("groups", None, None, None, None, "src", None, None),
        P("groups"),
        P("groups", None),
        P("groups", None),
        P("groups", None, "src", None),
        P("groups", None),
    )
    out_specs = P(("groups", "src"), None, None, None, None)
    return jax.shard_map(
        functools.partial(shards, mesh.shape["src"]),
        mesh=mesh, in_specs=in_specs, out_specs=out_specs, check_vma=False,
    )
```

```python
import functools

import jax
import jax.numpy as jnp
import numpy as np
from jax import lax
from jax.experimental import pallas as pl
from jax.experimental.pallas import tpu as pltpu
from jax.sharding import PartitionSpec as P

F32 = jnp.float32
BF16 = jnp.bfloat16
QUAD = 4


def site_tables(side_y, side_z):
    sites = side_y * side_z
    site = np.arange(sites)
    ypos, zpos = site // side_z, site % side_z
    up_y = ((ypos + 1) % side_y) * side_z + zpos
    up_z = ypos * side_z + (zpos + 1) % side_z
    masks, movers = [], []
    for target in (up_y, up_z):
        up = (target[:, None] == site[None, :]).astype(np.float32)
        masks += [up, up.T]
        movers += [up, np.eye(sites, dtype=np.float32)]
    masks = np.stack([np.tile(m, (1, 3)) for m in masks])
    movers = np.stack([np.kron(np.eye(3, dtype=np.float32), m) for m in movers])
    return masks, movers


def exchange_kernel(
    n, hops, owned_ref, hop_ref, pera_hbm, eig_hbm, links_hbm, masks_hbm, movers_hbm,
    blocks_ref, elem_ref,
    pera_ref, eig_ref, links_ref, masks_ref, movers_ref, fetch, pstage, epart, rows_ref, hopmask, estage, erecv, fstage, frecv,
    psend, precv, plocal, qsend, qrecv, zsend, zrecv,
):
    me = lax.axis_index("src")
    slots = blocks_ref.shape[0]
    time_count = eig_ref.shape[0]
    rings = n // QUAD
    mine_q, mine_z = lax.rem(me, QUAD), me // QUAD

    def listed(d, s):
        return jnp.minimum(jnp.maximum(owned_ref[s, d], 0), time_count - 1)

    pairs = (
        (pera_hbm, pera_ref), (eig_hbm, eig_ref), (links_hbm, links_ref),
        (masks_hbm, masks_ref), (movers_hbm, movers_ref),
    )
    fetches = [pltpu.make_async_copy(src, dst, fetch.at[i]) for i, (src, dst) in enumerate(pairs)]
    for copy in fetches:
        copy.start()

    barrier = pltpu.get_barrier_semaphore()

    @pl.loop(1, n)
    def _(o):
        pl.semaphore_signal(barrier, inc=1, device_id={"src": lax.rem(me + o, n)})

    fetches[0].wait()

    @pl.loop(0, n)
    def _(d):
        for s in range(slots):
            pstage[d, s] = pera_ref[listed(d, s)]

    pl.semaphore_wait(barrier, n - 1)

    def pera_copy(dz, dq, s, receive):
        peer = lax.rem(mine_z + dz, rings) * QUAD + lax.rem(mine_q + dq, QUAD)
        source = lax.rem(mine_z + rings - dz, rings) * QUAD + lax.rem(mine_q + QUAD - dq, QUAD)
        return pltpu.make_async_remote_copy(
            src_ref=pstage.at[peer, s], dst_ref=blocks_ref.at[s, source if receive else me],
            send_sem=psend.at[s, dz, dq], recv_sem=precv.at[s, dz, dq], device_id={"src": peer},
        )

    def local_copy(s):
        return pltpu.make_async_copy(pstage.at[me, s], blocks_ref.at[s, me], plocal.at[s])

    def send_slot(s):
        local_copy(s).start()

        @pl.loop(1, n)
        def _(o):
            pera_copy(o // QUAD, lax.rem(o, QUAD), s, False).start()

    def wait_slot(s):
        @pl.loop(0, rings - 1)
        def _(i):
            for dq in range(QUAD):
                pera_copy(i + 1, dq, s, True).wait()

        for dq in range(1, QUAD):
            pera_copy(0, dq, s, True).wait()
        local_copy(s).wait()

    for s in range(slots):
        local_copy(s).start()

    @pl.loop(1, n)
    def _(o):
        for s in range(slots):
            pera_copy(o // QUAD, lax.rem(o, QUAD), s, False).start()


    for copy in fetches[1:]:
        copy.wait()
    for h in range(hops):
        code = hop_ref[h]
        pick = [(code == i).astype(F32) for i in range(4)]
        hopmask[h] = sum(pick[i] * masks_ref[i] for i in range(4))
        mover = sum(pick[i] * movers_ref[i] for i in range(4)).astype(BF16)
        for k in range(2):
            sign = 1.0 - 2.0 * k
            for c in range(3):
                stack = []
                for d in range(3):
                    here, flip = k * 9 + c * 3 + d, k * 9 + d * 3 + c
                    stack.append(
                        pick[0] * links_ref[here].astype(F32)
                        + (sign * pick[1]) * links_ref[flip].astype(F32)
                        + pick[2] * links_ref[18 + here].astype(F32)
                        + (sign * pick[3]) * links_ref[18 + flip].astype(F32)
                    )
                rows_ref[h, k * 3 + c] = lax.dot_general(
                    jnp.concatenate(stack, 0).astype(BF16), mover, (((0,), (0,)), ((), ())),
                    preferred_element_type=F32,
                )

    def one_time(t, carry):
        vec = eig_ref[t]
        cur = vec
        half = vec.shape[0] // 2
        for h in range(hops):
            mask = hopmask[h]
            row = [rows_ref[h, i, pl.ds(t, 1), :] for i in range(6)]
            re = jnp.concatenate([mask * row[c] for c in range(3)], 0)
            im = jnp.concatenate([mask * row[3 + c] for c in range(3)], 0)
            re, im, neg = re.astype(BF16), im.astype(BF16), (-im).astype(BF16)
            top, low = cur[:half], cur[half:]
            out_re = jnp.dot(re, top, preferred_element_type=F32) + jnp.dot(neg, low, preferred_element_type=F32)
            out_im = jnp.dot(im, top, preferred_element_type=F32) + jnp.dot(re, low, preferred_element_type=F32)
            cur = jnp.concatenate([out_re, out_im], 0).astype(BF16)
        turned = jnp.concatenate([cur[half:], -cur[:half]], 0)
        both = jnp.concatenate([cur, turned], 1)
        part = lax.dot_general(vec, both, (((0,), (0,)), ((), ())), preferred_element_type=F32)
        epart[t] = part.astype(BF16)
        return carry

    lax.fori_loop(0, time_count, one_time, 0, unroll=4)

    @pl.loop(0, rings)
    def _(z):
        for q in range(QUAD):
            for s in range(slots):
                estage[q, z * slots + s] = epart[listed(z * QUAD + q, s)]

    def quad_copy(o, origin):
        peer = lax.rem(mine_q + o, QUAD)
        return pltpu.make_async_remote_copy(
            src_ref=estage.at[peer], dst_ref=erecv.at[origin],
            send_sem=qsend.at[o], recv_sem=qrecv.at[o], device_id={"src": mine_z * QUAD + peer},
        )

    for o in range(1, QUAD):
        quad_copy(o, mine_q).start()
    for o in range(1, QUAD):
        quad_copy(o, lax.rem(mine_q + QUAD - o, QUAD)).wait()

    @pl.loop(0, rings * slots)
    def _(j):
        total = estage[mine_q, j].astype(F32)
        for o in range(1, QUAD):
            total += erecv[lax.rem(mine_q + o, QUAD), j].astype(F32)
        fstage[j // slots, lax.rem(j, slots)] = total.astype(BF16)

    def ring_copy(o, origin):
        peer = lax.rem(mine_z + o, rings)
        return pltpu.make_async_remote_copy(
            src_ref=fstage.at[peer], dst_ref=frecv.at[origin],
            send_sem=zsend.at[o], recv_sem=zrecv.at[o], device_id={"src": peer * QUAD + mine_q},
        )

    for o in range(1, rings):
        ring_copy(o, mine_z).start()
    for o in range(1, rings):
        ring_copy(o, lax.rem(mine_z + rings - o, rings)).wait()
    total = fstage[mine_z].astype(F32)
    for o in range(1, rings):
        total += frecv[lax.rem(mine_z + o, rings)].astype(F32)
    elem_ref[...] = total.astype(BF16)

    for s in range(slots):
        wait_slot(s)


def triple_kernel(perm_ref, phase_ref, owned_ref, blocks_ref, elem_ref, out_ref, left, turned):
    slot, group = pl.program_id(0), pl.program_id(1)
    order = out_ref.shape[-1]
    width = elem_ref.shape[1]
    spins = order // width

    @pl.when(group == 0)
    def _():
        elem = elem_ref[0]
        re = blocks_ref[0, :, 0].reshape(order, order)
        im = blocks_ref[0, :, 1].reshape(order, order)
        left[:, :order] = re
        left[:, order:] = im
        for spin in range(spins):
            part_re = re[:, spin * width : (spin + 1) * width]
            part_im = im[:, spin * width : (spin + 1) * width]
            dims = (((1,), (1,)), ((), ()))
            turned[spin, 0] = lax.dot_general(
                elem, jnp.concatenate([part_re, -part_im], 1), dims, preferred_element_type=F32
            ).astype(BF16)
            turned[spin, 1] = lax.dot_general(
                elem, jnp.concatenate([part_im, part_re], 1), dims, preferred_element_type=F32
            ).astype(BF16)

    reals, imags = [], []
    for spin in range(spins):
        source = perm_ref[group, spin]
        phase = phase_ref[group, spin]
        scale_re = (phase == 0).astype(F32) - (phase == 2).astype(F32)
        scale_im = (phase == 1).astype(F32) - (phase == 3).astype(F32)
        re = turned[source, 0].astype(F32)
        im = turned[source, 1].astype(F32)
        reals.append((scale_re * re - scale_im * im).astype(BF16))
        imags.append((scale_re * im + scale_im * re).astype(BF16))
    real, imag = jnp.concatenate(reals, 0), jnp.concatenate(imags, 0)
    filled = owned_ref[slot, lax.axis_index("src")] >= 0
    lhs = left[...]
    for part, right in enumerate((jnp.concatenate([real, imag], 0), jnp.concatenate([imag, -real], 0))):
        result = jnp.dot(lhs, right, preferred_element_type=F32)
        out_ref[0, 0, part] = jnp.where(filled, result, 0.0).astype(BF16)


def shards(n, eigenvectors, gauge_links, hop_path, spin_perm, spin_phase, perambulators, owned_times):
    time_count = eigenvectors.shape[0]
    width = eigenvectors.shape[-1]
    slots = owned_times.shape[1]
    rows, order = perambulators.shape[2], perambulators.shape[3]
    groups = spin_perm.shape[0]
    hops = hop_path.shape[0]
    rings = n // QUAD
    side_y, side_z = eigenvectors.shape[4], eigenvectors.shape[5]
    sites = side_y * side_z
    eig = eigenvectors.reshape(time_count, -1, width)
    links = jnp.transpose(gauge_links.reshape(time_count, 36, sites), (1, 2, 0))
    masks, movers = site_tables(side_y, side_z)
    tile = (slots, width, 2 * width)
    vmem = pl.BlockSpec(memory_space=pltpu.VMEM)
    smem = pl.BlockSpec(memory_space=pltpu.SMEM)
    arrays = (perambulators, eig, links, jnp.asarray(masks), jnp.asarray(movers))
    blocks, elem = pl.pallas_call(
        functools.partial(exchange_kernel, n, hops),
        out_shape=(
            jax.ShapeDtypeStruct((slots, n, 2, rows, order), BF16),
            jax.ShapeDtypeStruct(tile, BF16),
        ),
        in_specs=[smem, smem] + [pl.BlockSpec(memory_space=pltpu.HBM)] * 5,
        out_specs=(pl.BlockSpec(memory_space=pl.ANY), vmem),
        scratch_shapes=[pltpu.VMEM(a.shape, a.dtype) for a in arrays]
        + [
            pltpu.SemaphoreType.DMA((len(arrays),)),
            pltpu.VMEM((n, slots, 2, rows, order), BF16),
            pltpu.VMEM((time_count, width, 2 * width), BF16),
            pltpu.VMEM((hops, 6, time_count, 3 * sites), F32),
            pltpu.VMEM((hops, sites, 3 * sites), F32),
            pltpu.VMEM((QUAD, rings * slots, width, 2 * width), BF16),
            pltpu.VMEM((QUAD, rings * slots, width, 2 * width), BF16),
            pltpu.VMEM((rings,) + tile, BF16),
            pltpu.VMEM((rings,) + tile, BF16),
            pltpu.SemaphoreType.DMA((slots, rings, QUAD)),
            pltpu.SemaphoreType.DMA((slots, rings, QUAD)),
            pltpu.SemaphoreType.DMA((slots,)),
            pltpu.SemaphoreType.DMA((QUAD,)),
            pltpu.SemaphoreType.DMA((QUAD,)),
            pltpu.SemaphoreType.DMA((rings,)),
            pltpu.SemaphoreType.DMA((rings,)),
        ],
        compiler_params=pltpu.CompilerParams(
            collective_id=0, has_side_effects=True, vmem_limit_bytes=56 * 2**20
        ),
        name="exchange",
    )(owned_times.T, hop_path, *arrays)
    return pl.pallas_call(
        triple_kernel,
        grid=(slots, groups),
        out_shape=jax.ShapeDtypeStruct((slots, groups, 2, order, order), BF16),
        in_specs=[
            smem,
            smem,
            smem,
            pl.BlockSpec((1, n, 2, rows, order), lambda s, g: (s, 0, 0, 0, 0)),
            pl.BlockSpec((1, width, 2 * width), lambda s, g: (s, 0, 0)),
        ],
        out_specs=pl.BlockSpec((1, 1, 2, order, order), lambda s, g: (s, g, 0, 0, 0)),
        scratch_shapes=[
            pltpu.VMEM((order, 2 * order), BF16),
            pltpu.VMEM((order // width, 2, width, order), BF16),
        ],
        compiler_params=pltpu.CompilerParams(
            dimension_semantics=("arbitrary", "arbitrary"), vmem_limit_bytes=56 * 2**20
        ),
        name="triple",
    )(spin_perm, spin_phase, owned_times.T, blocks, elem)


def solution(mesh):
    in_specs = (
        P("groups", None, None, "src", None, None, None),
        P("groups", None, None, None, None, "src", None, None),
        P("groups"),
        P("groups", None),
        P("groups", None),
        P("groups", None, "src", None),
        P("groups", None),
    )
    out_specs = P(("groups", "src"), None, None, None, None)
    return jax.shard_map(
        functools.partial(shards, mesh.shape["src"]),
        mesh=mesh, in_specs=in_specs, out_specs=out_specs, check_vma=False,
    )
```
